256 devices in a mesh: ctx: 64 (over y, x_hi, z), head: 4 (over x_lo, core).
Axes of the slice: x: 4 (x_hi: 2, x_lo: 2; x = x_hi * 2 + x_lo), y: 4, z: 8, core: 2. Of those that a mesh axis runs over, the one named last changes fastest.
Arguments:
- queries: float32 [8192, 32, 128], P('ctx', 'head'), may hold values from -8 to 8
- keys_in: float32 [8192, 4, 128], P('ctx', 'head'), may hold values from -8 to 8
- values: bfloat16 [8192, 4, 128], P('ctx', 'head'), may hold values from -6 to 6
- reflect_dirs: float32 [8192, 4, 128], P('ctx', 'head'), may hold values from -8 to 8
- out_proj: bfloat16 [4096, 4096], P('head'), may hold values from -0.125 to 0.125
Outputs:
- mixed: bfloat16 [8192, 4096], P('ctx', 'head')
The draws below stay inside these ranges and needn't reach their ends.
All inputs are finite; a program needn't handle non-finite values.
Results may differ from the reference program's by a relative error of at most 0.013.
The reference program's roundings to bfloat16 on the way (of `attended`) count: a program that leaves them out, or rounds other values in their place, can miss the bound.
Values may be sent and summed in bfloat16 or wider, within the bound.
No kernel may reach another device: no remote copies, remote signals or barrier semaphores. Data moves between devices by JAX's collectives and lax.ppermute only.
A program may use at most 64 MiB of HBM per device.

```python
import math
import jax
import jax.numpy as jnp
from jax import lax

HD = 128
QH = 32
KVH = 4
DOUT = 4096
TOK_DEV = 128
TOKENS = 8192
N_CTX = 64


def shared_fields(key):
    key_query, key_keys, key_dirs = jax.random.split(jax.random.fold_in(key, 7), 3)
    key_vals = jnp.clip(jax.random.normal(key_keys, (TOKENS, KVH, HD), jnp.float32), -4.0, 4.0)
    query_vals = jnp.clip(2.5 * jax.random.normal(key_query, (TOKENS, QH, HD), jnp.float32), -7.5, 7.5)
    dir_vals = jnp.clip(jax.random.normal(key_dirs, (TOKENS, KVH, HD), jnp.float32), -4.0, 4.0)
    return (query_vals, key_vals, dir_vals)


def draw_queries(key, part):
    return shared_fields(key)[0]


def draw_keys_in(key, part):
    return shared_fields(key)[1]


def draw_reflect_dirs(key, part):
    return shared_fields(key)[2]


def strengthened(values, stream_key, source, target, shards_of, factor):
    owner, partner = [(jnp.arange(values.shape[axis_at]) // (values.shape[axis_at] // shards_of)).reshape([-1 if axis == axis_at else 1 for axis in range(values.ndim)]) for axis_at in (source, target)]
    chosen = jax.random.permutation(stream_key, shards_of)[partner]
    strong = (owner == chosen) | (owner == (partner + shards_of // 2) % shards_of)
    return jnp.where(strong, factor * values, values)


def block_levels(key, extent, shards, smallest, top_value):
    def one(axis_at, shards_of):
        heights = jax.random.uniform(jax.random.fold_in(jax.random.fold_in(key, 6), axis_at), (shards_of,), jnp.float32, smallest / len(shards), top_value / len(shards))
        return jnp.repeat(jnp.exp(heights), extent[axis_at] // shards_of).reshape((-1,) + (1,) * (len(extent) - axis_at - 1))

    level = one(*shards[0])
    for cut in shards[1:]:
        level = level * one(*cut)
    return level


def normal_values(key, dims, scale, most, cuts=(), kind=jnp.bfloat16):
    drawn = jax.random.normal(key, dims, jnp.float32) * scale
    if len(cuts) > 0:
        drawn = block_levels(key, dims, cuts, -0.22, 0.18) * drawn
    return jnp.clip(drawn, min=-most, max=most).astype(kind)


def bell_draw_with(key, extent, scale, reach, pieces, heavy, held_as=jnp.bfloat16):
    drawn = scale * jax.random.normal(key, extent, jnp.float32)
    if pieces:
        drawn = drawn * block_levels(key, extent, pieces, -0.22, 0.18)
    return jnp.clip(strengthened(drawn, jax.random.fold_in(key, 3), *heavy), -reach, reach).astype(held_as)


def setup_inputs(seed: int = 0) -> dict:
    splits = jax.random.split(jax.random.key(seed), 6)
    return {
        "queries": draw_queries(jax.random.fold_in(splits[5], 71), 0),
        "keys_in": draw_keys_in(jax.random.fold_in(splits[5], 71), 0),
        "values": normal_values(splits[2], (TOKENS, KVH, HD), 1.0, 6.0, ((0, 64), (1, 4))),
        "reflect_dirs": draw_reflect_dirs(jax.random.fold_in(splits[5], 71), 0),
        "out_proj": bell_draw_with(splits[4], (QH * HD, DOUT), (QH * HD) ** -0.5, 0.125, ((0, 4),), (0, 1, 4, 2.0)),
    }


def chain_product(earlier, later):
    return jnp.einsum('...de,...ef->...df', earlier, later, precision=lax.Precision.HIGHEST)

def reflect_block(query_groups, keys_here, dirs_here):
    unit_dirs = dirs_here * lax.rsqrt(lax.optimization_barrier(jnp.sum(dirs_here * dirs_here, axis=-1, keepdims=True)) + 1e-06)
    rows_here = unit_dirs.shape[0]
    groups_here = unit_dirs.shape[1]
    head_size = unit_dirs.shape[2]
    gram_mat = jnp.einsum('jgd,kgd->gjk', unit_dirs, unit_dirs, precision=lax.Precision.HIGHEST)
    tri_inverse = jnp.triu(gram_mat, 1) + 0.5 * jnp.eye(rows_here, dtype=jnp.float32)
    stacked = jnp.concatenate([query_groups, keys_here[:, :, None]], axis=2)
    width_all = stacked.shape[2]
    projections = jnp.einsum('jgd,igcd->gjic', unit_dirs, stacked, precision=lax.Precision.HIGHEST)
    row_ids = jnp.arange(rows_here, dtype=jnp.int32)
    lower_mask = (row_ids[:, None] <= row_ids[None, :]).astype(jnp.float32)
    projections = projections * lower_mask[None, :, :, None]
    right_side = jnp.concatenate([jnp.transpose(unit_dirs, (1, 0, 2)), projections.reshape(groups_here, rows_here, rows_here * width_all)], axis=2)
    solved = jax.scipy.linalg.solve_triangular(tri_inverse, right_side, lower=False)
    z_rows = solved[:, :, :head_size]
    weights_back = solved[:, :, head_size:].reshape(groups_here, rows_here, rows_here, width_all)
    partial_moved = stacked - jnp.einsum('gjic,jgd->igcd', weights_back, unit_dirs, precision=lax.Precision.HIGHEST)
    ident_mat = jnp.eye(head_size, dtype=jnp.float32)[None]
    shard_product = ident_mat - jnp.einsum('jgd,gje->gde', unit_dirs, z_rows, precision=lax.Precision.HIGHEST)
    return (partial_moved, shard_product)

def reference(queries, keys_in, values, reflect_dirs, out_proj):
    per_group = QH // KVH
    q_blocks = queries.reshape(N_CTX, TOK_DEV, KVH, per_group, HD)
    k_blocks = keys_in.reshape(N_CTX, TOK_DEV, KVH, HD)
    d_blocks = reflect_dirs.reshape(N_CTX, TOK_DEV, KVH, HD)

    def advance(before, bundle):
        q_here, k_here, d_here = bundle
        partial_moved, shard_product = reflect_block(q_here, k_here, d_here)
        rotated = jnp.einsum('gde,igce->igcd', before, partial_moved, precision=lax.Precision.HIGHEST)
        return (chain_product(before, shard_product), rotated)
    ident_all = jnp.broadcast_to(jnp.eye(HD, dtype=jnp.float32), (KVH, HD, HD))
    _, rotated = lax.scan(advance, ident_all, (q_blocks, k_blocks, d_blocks))
    rotated = rotated.reshape(TOKENS, KVH, per_group + 1, HD)
    query_turned = lax.optimization_barrier(rotated[:, :, :per_group].astype(jnp.bfloat16)).astype(jnp.float32)
    key_turned = lax.optimization_barrier(rotated[:, :, per_group].astype(jnp.bfloat16)).astype(jnp.float32)
    value_full = values.astype(jnp.float32)
    block_len = math.gcd(TOKENS, 1024)
    n_blocks = TOKENS // block_len
    inv_sqrt = 1.0 / math.sqrt(HD)

    def query_block(block_index):
        q_piece = lax.dynamic_slice_in_dim(query_turned, block_index * block_len, block_len, 0)
        query_pos = block_index * block_len + jnp.arange(block_len, dtype=jnp.int32)
        peak0 = jnp.full((block_len, KVH, per_group), -1e+30, jnp.float32)
        denom0 = jnp.zeros((block_len, KVH, per_group), jnp.float32)
        numer0 = jnp.zeros((block_len, KVH, per_group, HD), jnp.float32)

        def visit(key_index, running):
            peak, denom, numer = running
            k_piece = lax.dynamic_slice_in_dim(key_turned, key_index * block_len, block_len, 0)
            v_piece = lax.dynamic_slice_in_dim(value_full, key_index * block_len, block_len, 0)
            key_pos = key_index * block_len + jnp.arange(block_len, dtype=jnp.int32)
            allowed = (key_pos[None, :] <= query_pos[:, None])[:, None, None, :]
            scores = jnp.einsum('tgrd,sgd->tgrs', q_piece, k_piece) * inv_sqrt
            scores = jnp.where(allowed, scores, -1e+30)
            new_peak = jnp.maximum(peak, lax.optimization_barrier(jnp.max(scores, axis=-1)))
            weights = jnp.where(allowed, jnp.exp(scores - new_peak[..., None]), 0.0)
            shrink = jnp.exp(peak - new_peak)
            denom = denom * shrink + lax.optimization_barrier(jnp.sum(weights, axis=-1))
            low_weights = lax.optimization_barrier(weights.astype(jnp.bfloat16)).astype(jnp.float32)
            numer = numer * shrink[..., None] + jnp.einsum('tgrs,sgd->tgrd', low_weights, v_piece)
            return (new_peak, denom, numer)
        peak, denom, numer = lax.fori_loop(0, block_index + 1, visit, (peak0, denom0, numer0))
        return (numer / denom[..., None]).astype(jnp.bfloat16)
    attended = lax.map(query_block, jnp.arange(n_blocks, dtype=jnp.int32))
    attended = attended.reshape(TOKENS, QH * HD)
    return jnp.dot(attended.astype(jnp.float32), out_proj.astype(jnp.float32), preferred_element_type=jnp.float32).astype(jnp.bfloat16)
```

```python
import functools
import math

import jax
import jax.numpy as jnp
from jax import lax
from jax.experimental import pallas as pl
from jax.experimental.pallas import tpu as pltpu
from jax.sharding import PartitionSpec as P

NZ = 8
NG = 8
T = 128
R = 8
HD = 128
ROWS = T * R
GT = NZ * T
NEG = -1e30
HI = lax.Precision.HIGHEST
LOG2E = 1.4426950408889634
ZGROUPS = [[g * NZ + i for i in range(NZ)] for g in range(NG)]
YXGROUPS = [[g * NZ + i for g in range(NG)] for i in range(NZ)]


VMEM = pl.BlockSpec(memory_space=pltpu.VMEM)
HBM = pl.BlockSpec(memory_space=pltpu.HBM)
SMEM = pl.BlockSpec(memory_space=pltpu.SMEM)


def params(**kw):
    return pltpu.CompilerParams(vmem_limit_bytes=48 * 1024 * 1024, **kw)


def mm(a, b):
    return lax.dot_general(a, b, (((1,), (0,)), ((), ())), precision=HI,
                           preferred_element_type=jnp.float32)


def mm_nt(a, b):
    return lax.dot_general(a, b, (((1,), (1,)), ((), ())), precision=HI,
                           preferred_element_type=jnp.float32)


def mm_tn(a, b):
    return lax.dot_general(a, b, (((0,), (0,)), ((), ())), precision=HI,
                           preferred_element_type=jnp.float32)


def split(x):
    hi = x.astype(jnp.bfloat16)
    lo = (x - hi.astype(jnp.float32)).astype(jnp.bfloat16)
    return hi, lo


def mm3(a, b):
    ah, al = split(a)
    bh, bl = split(b)
    left = jnp.concatenate([ah, al], axis=1)
    right = jnp.concatenate([bh, bh], axis=0)
    return (jnp.dot(left, right, preferred_element_type=jnp.float32)
            + jnp.dot(ah, bl, preferred_element_type=jnp.float32))


def iota2(shape, dim):
    return lax.broadcasted_iota(jnp.int32, shape, dim)


def copies_out(src_ref, dst_ref, sem, count):
    cs = [pltpu.make_async_copy(src_ref, dst_ref.at[i], sem.at[i]) for i in range(count)]
    for c in cs:
        c.start()
    for c in cs:
        c.wait()


def spread_kernel(v_ref, o_ref, sem):
    copies_out(v_ref, o_ref, sem, NZ)


def spread(v):
    return pl.pallas_call(
        spread_kernel,
        out_shape=jax.ShapeDtypeStruct((NZ,) + v.shape, v.dtype),
        in_specs=[VMEM], out_specs=HBM,
        scratch_shapes=[pltpu.SemaphoreType.DMA((NZ,))],
        compiler_params=params(),
        name="spread",
    )(v)


def reflect_kernel(q_ref, k_ref, d_ref, qm_ref, m_ref, km_ref, kbuf, sem):
    d = d_ref[...]
    u = d * lax.rsqrt(jnp.sum(d * d, axis=-1, keepdims=True) + 1e-6)
    row, col = iota2((T, T), 0), iota2((T, T), 1)
    eye = (row == col).astype(jnp.float32)
    gram = mm_nt(u, u)
    upper = jnp.where(col > row, gram, 0.0)
    size = 1
    inv = 2.0 * eye
    while size < T:
        corner = ((row // (2 * size)) == (col // (2 * size))) & ((row // size) % 2 == 0) & ((col // size) % 2 == 1)
        part = jnp.where(corner, upper, 0.0)
        if size == 1:
            inv = inv - 4.0 * part
        else:
            inv = inv - mm(inv, mm(part, inv))
        size *= 2
    z = mm_tn(inv, u)
    m_ref[...] = eye - mm_tn(z, u)
    k = k_ref[...]
    pk = jnp.where(col <= row, mm_nt(k, u), 0.0)
    kbuf[...] = k - mm(pk, z)
    cs = [pltpu.make_async_copy(kbuf, km_ref.at[i], sem.at[i]) for i in range(NZ)]
    for c in cs:
        c.start()
    ut = u.T
    for b in range(0, ROWS, 256):
        q = q_ref[b:b + 256, :]
        pq = mm3(q, ut)
        keep = iota2((256, T), 1) <= (iota2((256, T), 0) + b) // R
        pq = jnp.where(keep, pq, 0.0)
        qm_ref[b:b + 256, :] = q - mm3(pq, z)
    for c in cs:
        c.wait()


def reflect(q, k, d):
    return pl.pallas_call(
        reflect_kernel,
        out_shape=(jax.ShapeDtypeStruct((ROWS, HD), jnp.float32),
                   jax.ShapeDtypeStruct((HD, HD), jnp.float32),
                   jax.ShapeDtypeStruct((NZ, T, HD), jnp.float32)),
        in_specs=[VMEM, VMEM, VMEM], out_specs=(VMEM, VMEM, HBM),
        scratch_shapes=[pltpu.VMEM((T, HD), jnp.float32), pltpu.SemaphoreType.DMA((NZ,))],
        compiler_params=params(),
        name="reflect",
    )(q, k, d)


def prefixes(m):
    p01, p23, p45, p67 = [mm(m[i], m[i + 1]) for i in (0, 2, 4, 6)]
    p012, p0123 = mm(p01, m[2]), mm(p01, p23)
    p456, p4567 = mm(p45, m[6]), mm(p45, p67)
    return [m[0], p01, p012, p0123, mm(p0123, m[4]), mm(p0123, p45), mm(p0123, p456), mm(p0123, p4567)]


def inner_kernel(m_ref, b_ref, g_ref):
    ps = prefixes([m_ref[i] for i in range(NZ)])
    row, col = iota2((HD, HD), 0), iota2((HD, HD), 1)
    b_ref[0] = (row == col).astype(jnp.float32)
    for i in range(NZ - 1):
        b_ref[i + 1] = ps[i]
    g_ref[...] = ps[-1]


def inner_prefix(m):
    return pl.pallas_call(
        inner_kernel,
        out_shape=(jax.ShapeDtypeStruct((NZ, HD, HD), jnp.float32),
                   jax.ShapeDtypeStruct((HD, HD), jnp.float32)),
        in_specs=[VMEM], out_specs=(VMEM, VMEM),
        compiler_params=params(),
        name="inner_prefix",
    )(m)


def turn_kernel(pos_ref, g_ref, b_ref, q_ref, k_ref, qt_ref, kt_ref, abuf):
    group, place = pos_ref[0], pos_ref[1]
    ps = prefixes([g_ref[i] for i in range(NG)])
    row, col = iota2((HD, HD), 0), iota2((HD, HD), 1)
    abuf[0] = (row == col).astype(jnp.float32)
    for i in range(NG - 1):
        abuf[i + 1] = ps[i]
    a = abuf[group]
    mine = mm(a, b_ref[place]).T
    for b in range(0, ROWS, 256):
        qt_ref[b:b + 256, :] = mm3(q_ref[b:b + 256, :], mine).astype(jnp.bfloat16)
    for i in range(NZ):
        ab = mm(a, b_ref[i]) if i else a
        kt_ref[i * T:(i + 1) * T, :] = mm_nt(k_ref[i], ab).astype(jnp.bfloat16)


def turn(pos, g, b, q, k):
    return pl.pallas_call(
        turn_kernel,
        out_shape=(jax.ShapeDtypeStruct((ROWS, HD), jnp.bfloat16),
                   jax.ShapeDtypeStruct((GT, HD), jnp.bfloat16)),
        in_specs=[SMEM, VMEM, VMEM, VMEM, VMEM], out_specs=(VMEM, VMEM),
        scratch_shapes=[pltpu.VMEM((NG, HD, HD), jnp.float32)],
        compiler_params=params(),
        name="turn",
    )(pos, g, b, q, k)


QT = 256
SCALE2 = LOG2E / math.sqrt(HD)


def softmax_step(q, k, v, m_old, l_old, acc_old, keep):
    s = lax.dot_general(q, k, (((1,), (1,)), ((), ())), preferred_element_type=jnp.float32)
    s = s * SCALE2
    if keep is not None:
        s = jnp.where(keep, s, NEG)
    m_new = jnp.maximum(m_old, jnp.max(s, axis=-1, keepdims=True))
    p = jnp.exp2(s - m_new)
    if keep is not None:
        p = jnp.where(keep, p, 0.0)
    shrink = jnp.exp2(m_old - m_new)
    l_new = l_old * shrink + jnp.sum(p, axis=-1, keepdims=True)
    acc_new = acc_old * shrink + jnp.dot(p.astype(jnp.bfloat16), v, preferred_element_type=jnp.float32)
    return m_new, l_new, acc_new


def own_kernel(pos_ref, q_ref, k_ref, v_ref, m_ref, l_ref, acc_ref):
    place = pos_ref[1]
    start = pl.multiple_of(place * T, T)
    for b in range(0, ROWS, QT):
        rows = slice(b, b + QT)
        keep = iota2((QT, T), 1) <= (iota2((QT, T), 0) + b) // R
        m, l, acc = softmax_step(
            q_ref[rows, :], k_ref[pl.ds(start, T), :], v_ref[pl.ds(start, T), :],
            jnp.full((QT, 1), NEG, jnp.float32), jnp.zeros((QT, 1), jnp.float32),
            jnp.zeros((QT, HD), jnp.float32), keep)
        m_ref[rows, :], l_ref[rows, :], acc_ref[rows, :] = m, l, acc

    def body(j, carry):
        at = pl.multiple_of(j * T, T)
        for b in range(0, ROWS, QT):
            rows = slice(b, b + QT)
            m, l, acc = softmax_step(
                q_ref[rows, :], k_ref[pl.ds(at, T), :], v_ref[pl.ds(at, T), :],
                m_ref[rows, :], l_ref[rows, :], acc_ref[rows, :], None)
            m_ref[rows, :], l_ref[rows, :], acc_ref[rows, :] = m, l, acc
        return carry

    lax.fori_loop(0, place, body, 0)


STATE = (jax.ShapeDtypeStruct((ROWS, 1), jnp.float32),
         jax.ShapeDtypeStruct((ROWS, 1), jnp.float32),
         jax.ShapeDtypeStruct((ROWS, HD), jnp.float32))


def attend_own(pos, q, k, v):
    return pl.pallas_call(
        own_kernel,
        out_shape=STATE,
        in_specs=[SMEM, VMEM, VMEM, VMEM], out_specs=(VMEM, VMEM, VMEM),
        compiler_params=params(),
        cost_estimate=pl.CostEstimate(flops=2 * 2 * ROWS * GT * HD, bytes_accessed=2 << 20, transcendentals=ROWS * GT),
        name="attend_own",
    )(pos, q, k, v)


KB = 512


def far_kernel(last, live_ref, q_ref, k_ref, v_ref, m_in, l_in, acc_in, *outs):
    if last:
        out_ref, m_ref, l_ref, acc_ref = outs
    else:
        m_ref, l_ref, acc_ref = outs
    blocks = k_ref.shape[0] // KB
    m_ref[...], l_ref[...], acc_ref[...] = m_in[...], l_in[...], acc_in[...]

    def body(j, carry):
        at = pl.multiple_of(j * KB, KB)
        for b in range(0, ROWS, QT):
            rows = slice(b, b + QT)
            m, l, acc = softmax_step(
                q_ref[rows, :], k_ref[pl.ds(at, KB), :], v_ref[pl.ds(at, KB), :],
                m_ref[rows, :], l_ref[rows, :], acc_ref[rows, :], None)
            m_ref[rows, :], l_ref[rows, :], acc_ref[rows, :] = m, l, acc
        return carry

    lax.fori_loop(0, live_ref[0] * blocks, body, 0)
    if last:
        out_ref[...] = (acc_ref[...] / l_ref[...]).astype(jnp.bfloat16)


def attend_far(live, q, k, v, state, last=False):
    n = k.shape[0]
    return pl.pallas_call(
        functools.partial(far_kernel, last),
        out_shape=jax.ShapeDtypeStruct((ROWS, HD), jnp.bfloat16) if last else STATE,
        in_specs=[SMEM] + [VMEM] * 6, out_specs=VMEM if last else (VMEM, VMEM, VMEM),
        scratch_shapes=[pltpu.VMEM(s.shape, s.dtype) for s in STATE] if last else [],
        compiler_params=params(),
        cost_estimate=pl.CostEstimate(flops=2 * 2 * ROWS * n * HD, bytes_accessed=2 << 20, transcendentals=ROWS * n),
        name="attend_far",
    )(live, q, k, v, *state)


def over_z(x):
    return lax.all_to_all(x, "ctx", 0, 0, axis_index_groups=ZGROUPS)


def y_shift(d):
    return [(s, (s + 16 * d) % 64) for s in range(64)]


def shards(queries, keys_in, values, reflect_dirs, out_proj):
    me = lax.axis_index("ctx").astype(jnp.int32)
    head = lax.axis_index("head").astype(jnp.int32)
    group, place = me // NZ, me % NZ
    y, xh = group // 2, group % 2
    pos = jnp.stack([group, place])
    q_in = queries.reshape(ROWS, HD)
    k_in = keys_in.reshape(T, HD)
    d_in = reflect_dirs.reshape(T, HD)
    v_in = values.reshape(T, HD)

    swap_x = [(s, s ^ 8) for s in range(64)]
    v_own = over_z(spread(v_in)).reshape(GT, HD)
    qm, m, km = reflect(q_in, k_in, d_in)
    v_x = lax.ppermute(v_own, "ctx", swap_x)
    m_all = over_z(jnp.broadcast_to(m[None], (NZ, HD, HD)))
    b_all, g = inner_prefix(m_all)
    k_all = over_z(km)
    g_all = lax.all_to_all(jnp.broadcast_to(g[None], (NG, HD, HD)), "ctx", 0, 0, axis_index_groups=YXGROUPS)
    q_low, k_own = turn(pos, g_all, b_all, qm, k_all)
    k_x = lax.ppermute(k_own, "ctx", swap_x)
    v_pair = jnp.concatenate([v_own, v_x], axis=0)
    v_far = [lax.ppermute(v_pair, "ctx", y_shift(d)) for d in (1, 3, 2)]
    k_pair = jnp.concatenate([k_own, k_x], axis=0)
    k_far = [lax.ppermute(k_pair, "ctx", y_shift(d)) for d in (1, 3, 2)]
    state = attend_own(pos, q_low, k_own, v_own)
    state = attend_far(xh[None], q_low, k_x, v_x, state)
    for i, d in enumerate((1, 3, 2)):
        live = (y >= d).astype(jnp.int32)[None]
        state = attend_far(live, q_low, k_far[i], v_far[i], state, last=i == 2)
    attended = state.reshape(T, R * HD)
    part = jnp.dot(attended, out_proj, preferred_element_type=jnp.float32).astype(jnp.bfloat16)
    part = part.reshape(T, 2, 2, 1024)
    core, xlo = head % 2, head // 2
    keep1 = lax.dynamic_index_in_dim(part, core, 2, False)
    send1 = lax.dynamic_index_in_dim(part, 1 - core, 2, False)
    got1 = lax.ppermute(send1, "head", [(s, s ^ 1) for s in range(4)])
    sum1 = keep1.astype(jnp.float32) + got1.astype(jnp.float32)
    keep2 = lax.dynamic_index_in_dim(sum1, xlo, 1, False)
    send2 = lax.dynamic_index_in_dim(sum1, 1 - xlo, 1, False).astype(jnp.bfloat16)
    got2 = lax.ppermute(send2, "head", [(s, s ^ 2) for s in range(4)])
    return (keep2 + got2.astype(jnp.float32)).astype(jnp.bfloat16)


def solution(mesh):
    return jax.shard_map(
        shards,
        mesh=mesh,
        in_specs=(
            P("ctx", "head", None),
            P("ctx", "head", None),
            P("ctx", "head", None),
            P("ctx", "head", None),
            P("head", None),
        ),
        out_specs=P("ctx", "head"),
        check_vma=False,
    )
```
